1024 devices in a mesh: gx: 8 (over x, core), gy: 16 (over z_lo), gz: 8 (over y, z_hi).
Axes of the slice: x: 4, y: 4, z: 32 (z_hi: 2, z_lo: 16; z = z_hi * 16 + z_lo), core: 2. Of those that a mesh axis runs over, the one named last changes fastest.
Arguments:
- schur: bfloat16 [8, 16, 8, 1024, 1024], P('gx', 'gy', 'gz'), may hold values from -10 to 10, as said below
- rhs_local: float32 [8, 16, 8, 32, 1024], P('gx', 'gy', 'gz'), may hold values from -40 to 40
- block_map: int32 [8, 16, 8, 8], P('gx', 'gy', 'gz'), may hold values from 0 to 7, each once within a row
Outputs:
- solution: float32 [8, 16, 8, 32, 1024], P('gx', 'gy', 'gz')
- residual: float32 [8, 16, 8, 32, 1024], P('gx', 'gy', 'gz')
The draws below stay inside these ranges and needn't reach their ends.
Inputs may be any that keep to these rules, and one draw needn't show every extreme that they name: `schur`: each local Schur complement is symmetric positive definite.
All inputs are finite; a program needn't handle non-finite values.
Results may differ from the reference program's by a relative error of at most 0.0003.
Values sent between devices are 32-bit elements; how exact they have to be, the bound alone decides.
No kernel may reach another device: no remote copies, remote signals or barrier semaphores. Data moves between devices by JAX's collectives and lax.ppermute only.
A program may use at most 64 MiB of HBM per device.

```python
import math
import jax
import jax.numpy as jnp
from jax import lax

B = 128
M = 1024
R = 32
NGX = 8
NGY = 16
NGZ = 8


def draw_schur(key, part):
    keys = jax.random.split(key, NGX * NGY * NGZ)

    def one(single):
        key_a, key_b, key_c, key_d = jax.random.split(single, 4)
        small_q = jnp.linalg.qr(jax.random.normal(key_a, (8, 8), jnp.float32))[0]
        large_q = jnp.linalg.qr(jax.random.normal(key_b, (B, B), jnp.float32))[0]
        uniform_u = jax.random.uniform(key_c, (M - 2,), jnp.float32, 0.0, 1.0)
        lowest = 10.0 / 300.0
        inner_lam = 10.0 * jnp.exp(-math.log(300.0) * uniform_u)
        spectrum = jnp.concatenate([jnp.array([10.0, lowest], jnp.float32), inner_lam])
        basis = jnp.kron(small_q, large_q)
        scaled = (spectrum[:, None] * basis.T).reshape((8, B, M))
        mixed = jnp.einsum('ia,jb,abm->ijm', small_q, large_q, scaled, precision=lax.Precision.HIGHEST).reshape((M, M))
        mixed = 0.5 * (mixed + mixed.T)
        order = jax.random.permutation(key_d, M)
        mixed = jnp.take(jnp.take(mixed, order, axis=0), order, axis=1)
        return jnp.clip(mixed, -10.0, 10.0).astype(jnp.bfloat16)
    return lax.map(one, keys).reshape((NGX, NGY, NGZ, M, M))


def draw_rhs_local(key, part):
    base = jnp.clip(jax.random.normal(key, (NGX, NGY, NGZ, R, M), jnp.float32), -6.0, 6.0)
    ramp = 1.0 + 2.0 * jnp.arange(NGX, dtype=jnp.float32) / max(NGX - 1, 1)
    ramp = ramp.reshape((NGX, 1, 1, 1, 1))
    values = base * ramp
    return jnp.clip(values, -40.0, 40.0)


def setup_inputs(seed: int = 0) -> dict:
    splits = jax.random.split(jax.random.key(seed), 4)
    return {
        "schur": draw_schur(jax.random.fold_in(splits[3], 71), 0),
        "rhs_local": draw_rhs_local(jax.random.fold_in(splits[3], 71), 0),
        "block_map": jax.vmap(lambda own: jax.random.permutation(own, 8))(jax.random.split(splits[2], NGX * NGY * NGZ)).reshape((NGX, NGY, NGZ, 8)).astype(jnp.int32),
    }


def solve_spd(gram_mat, right):
    lower = jnp.linalg.cholesky(gram_mat)
    step_one = lax.linalg.triangular_solve(lower, right, left_side=True, lower=True)
    return lax.linalg.triangular_solve(lower, step_one, left_side=True, lower=True, transpose_a=True)

def apply_factor(factor, vect):
    step_one = lax.linalg.triangular_solve(factor, vect, left_side=False, lower=True, transpose_a=True)
    return lax.linalg.triangular_solve(factor, step_one, left_side=False, lower=True, transpose_a=False)

def build_bar(local, starts, over):
    for face in range(6):
        pos = starts[face].astype(jnp.int32)
        block = lax.dynamic_slice(local, (pos, pos), (B, B))
        local = lax.dynamic_update_slice(local, block + over[face], (pos, pos))
    return local

def below(array, axis):
    first = jnp.zeros_like(lax.slice_in_dim(array, 0, 1, axis=axis))
    rest = lax.slice_in_dim(array, 0, array.shape[axis] - 1, axis=axis)
    return jnp.concatenate([first, rest], axis=axis)

def above(array, axis):
    last = jnp.zeros_like(lax.slice_in_dim(array, 0, 1, axis=axis))
    rest = lax.slice_in_dim(array, 1, array.shape[axis], axis=axis)
    return jnp.concatenate([rest, last], axis=axis)

def partners(faces):
    parts_in = [below(faces[:, :, :, 1], 0), above(faces[:, :, :, 0], 0), below(faces[:, :, :, 3], 1), above(faces[:, :, :, 2], 1), below(faces[:, :, :, 5], 2), above(faces[:, :, :, 4], 2)]
    return jnp.stack(parts_in, axis=3)

def reference(schur, rhs_local, block_map):
    grid = schur.shape[:3]
    count = grid[0] * grid[1] * grid[2]
    starts = (block_map[..., :6] * B).astype(jnp.int32)
    onehot = (block_map[..., :6, None] == jnp.arange(8, dtype=jnp.int32)).astype(rhs_local.dtype)
    flat_s = schur.reshape((count, M, M))
    flat_st = starts.reshape((count, 6))

    def cut_faces(vect):
        blocks = vect.reshape(grid + (vect.shape[3], 8, B))
        index = block_map[..., None, :6, None]
        taken = jnp.take_along_axis(blocks, index, axis=-2)
        return jnp.moveaxis(taken, -2, -3)

    def spread(recv):
        rows = recv.shape[4]
        added = jnp.einsum('xyzfp,xyzfab->xyzapb', onehot, recv, precision=lax.Precision.HIGHEST)
        return added.reshape(grid + (rows, M))

    def assemble(vect):
        return vect + spread(partners(cut_faces(vect)))

    def diag_blocks(item):
        local = item[0].astype(jnp.float32)
        return jnp.stack([lax.dynamic_slice(local, (item[1][f], item[1][f]), (B, B)) for f in range(6)])
    blocks = lax.map(diag_blocks, (flat_s, flat_st)).reshape(grid + (6, B, B))
    over = partners(blocks).reshape((count, 6, B, B))

    def precond(vect):

        def one(item):
            local = build_bar(item[0].astype(jnp.float32), item[1], item[2])
            factor = jnp.linalg.cholesky(local)
            return apply_factor(factor, item[3])
        out = lax.map(one, (flat_s, flat_st, over, vect.reshape((count, R, M))))
        return assemble(out.reshape(grid + (R, M)))

    def matvec(vect):

        def one(item):
            return jnp.dot(item[1], item[0].astype(jnp.float32), precision=lax.Precision.HIGHEST)
        out = lax.map(one, (flat_s, vect.reshape((count, R, M))))
        return assemble(out.reshape(grid + (R, M)))
    ix = jnp.arange(grid[0], dtype=jnp.int32)[:, None, None]
    iy = jnp.arange(grid[1], dtype=jnp.int32)[None, :, None]
    iz = jnp.arange(grid[2], dtype=jnp.int32)[None, None, :]
    present = jnp.stack([ix > 0 + 0 * iy * iz, (ix < grid[0] - 1) + 0 * iy * iz, (iy > 0) + 0 * ix * iz, (iy < grid[1] - 1) + 0 * ix * iz, (iz > 0) + 0 * ix * iy, (iz < grid[2] - 1) + 0 * ix * iy], axis=-1)
    present = jnp.broadcast_to(present, grid + (6,)).astype(rhs_local.dtype)
    half = jnp.einsum('xyzfp,xyzf->xyzp', onehot, present, precision=lax.Precision.HIGHEST)
    weights = jnp.broadcast_to((1.0 - 0.5 * half)[..., None], grid + (8, B)).reshape(grid + (1, M))

    def inner(left, right):
        return jnp.einsum('xyzam,xyzbm->ab', left * weights, right, precision=lax.Precision.HIGHEST)

    def combine(coef, vect):
        return jnp.einsum('ab,xyzam->xyzbm', coef, vect, precision=lax.Precision.HIGHEST)
    residual = assemble(rhs_local)
    zeta = precond(residual)
    rho_now = inner(zeta, residual)
    image = matvec(zeta)
    alpha = solve_spd(inner(zeta, image), rho_now)
    solution = combine(alpha, zeta)
    residual = residual - combine(alpha, image)
    return (solution, residual)
```

```python
import functools

import jax
import jax.numpy as jnp
from jax import lax
from jax.experimental import pallas as pl
from jax.experimental.pallas import tpu as pltpu
from jax.sharding import PartitionSpec as P

B = 128
M = 1024
R = 32
F32 = jnp.float32
HIGHEST = lax.Precision.HIGHEST
ORDER = (6, 7, 0, 1, 2, 3, 4, 5)
PANEL = 2 * B
GROUPS = 2
VMEM = pl.BlockSpec(memory_space=pltpu.VMEM)
SMEM = pl.BlockSpec(memory_space=pltpu.SMEM)


def mm(a, b, dims=((1,), (0,))):
    return lax.dot_general(
        a, b, (dims, ((), ())), precision=HIGHEST, preferred_element_type=F32
    )


def mmt(a, b):
    return mm(a, b, ((1,), (1,)))


def block(pos):
    return pl.ds(pl.multiple_of(pos * B, B), B)


def pivot_pair(rows, p, lane, sub):
    group, s = divmod(p, 8)
    r0 = rows[group][s : s + 1, :]
    r1 = rows[group][s + 1 : s + 2, :]
    a, b, c = r0[:, p : p + 1], r0[:, p + 1 : p + 2], r1[:, p + 1 : p + 2]
    scale = 1.0 / (a * c - b * b)
    i00, i01, i11 = c * scale, -b * scale, a * scale
    first, second = lane == p, lane == p + 1
    either = first | second
    n0 = jnp.where(first[:1], i00, jnp.where(second[:1], i01, i00 * r0 + i01 * r1))
    n1 = jnp.where(first[:1], i01, jnp.where(second[:1], i11, i01 * r0 + i11 * r1))
    new = []
    for v, old in enumerate(rows):
        out = jnp.where(either, 0.0, old) - old[:, p : p + 1] * n0 - old[:, p + 1 : p + 2] * n1
        if v == group:
            out = jnp.where(sub == s, n0, jnp.where(sub == s + 1, n1, out))
        new.append(out)
    return new


def inverse(rows):
    lane = lax.broadcasted_iota(jnp.int32, (8, B), 1)
    sub = lax.broadcasted_iota(jnp.int32, (8, B), 0)

    def body(_, carry):
        rows = list(carry)
        for p in range(0, 8 * GROUPS, 2):
            rows = pivot_pair(rows, p, lane, sub)
        rows = rows[GROUPS:] + rows[:GROUPS]
        return tuple(pltpu.roll(row, B - 8 * GROUPS, 1) for row in rows)

    return lax.fori_loop(0, 16 // GROUPS, body, tuple(rows))


def inverse_of(ref, row, col, out):
    rows = [ref[row + 8 * v : row + 8 * v + 8, col : col + B] for v in range(16)]
    for v, value in enumerate(inverse(rows)):
        out[8 * v : 8 * v + 8, :] = value


def eliminate(panel, kept, inv):
    inverse_of(panel, 0, 0, inv)
    below = panel[B:, :B]
    scaled = mm(below, inv[...])
    kept[B : panel.shape[0], :B] = below
    panel[B:, :B] = scaled
    panel[B:, B:] -= mmt(scaled, below[:B])
    inverse_of(panel, B, B, inv)
    below = panel[PANEL:, B:]
    kept[PANEL : panel.shape[0], B:] = below
    panel[PANEL:, B:] = mm(below, inv[...])


def update(panel, kept, later, gap):
    later[...] -= mmt(panel[PANEL * gap :, :], kept[PANEL * gap : PANEL * (gap + 1), :])


def pack_kernel(map_ref, schur_ref, rhs_ref, *sends):
    for face in range(6):
        at = block(map_ref[face])
        sends[face][:B, :] = schur_ref[at, at].astype(F32)
        sends[face][B:, :] = rhs_ref[:, at]


def first_kernel(map_ref, schur_ref, rhs_ref, c0, c1, c2, c3, kept, inv):
    panels = (c0, c1, c2, c3)
    for j in range(8):
        panel, left = panels[j // 2], (j % 2) * B
        col = block(map_ref[ORDER[j]])
        for i in range(j // 2 * 2, 8):
            top = (i - j // 2 * 2) * B
            panel[top : top + B, left : left + B] = schur_ref[
                block(map_ref[ORDER[i]]), col
            ].astype(F32)
        panel[panel.shape[0] - R :, left : left + B] = rhs_ref[:, col]
    eliminate(c0, kept, inv)
    for gap in (1, 2, 3):
        update(c0, kept, panels[gap], gap)


def add_received(panel, half, received):
    rows = slice(half * B, half * B + B)
    panel[rows, rows] += received[:B, :]
    panel[panel.shape[0] - R :, rows] += received[B:, :]


def middle_kernel(i1, i2, i3, x0, x1, y0, y1, c1, c2, c3, kept, inv):
    c1[...], c2[...], c3[...] = i1[...], i2[...], i3[...]
    for panel, pair in ((c1, (x0, x1)), (c2, (y0, y1))):
        for half in range(2):
            add_received(panel, half, pair[half])
    eliminate(c1, kept, inv)
    update(c1, kept, c2, 1)
    update(c1, kept, c3, 2)
    eliminate(c2, kept, inv)
    update(c2, kept, c3, 1)


def last_kernel(c0, c1, c2, i3, z0, z1, zeta, *rest):
    sends, (c3, kept, inv) = rest[:6], rest[6:]
    c3[...] = i3[...]
    add_received(c3, 0, z0)
    add_received(c3, 1, z1)
    eliminate(c3, kept, inv)
    for step in (3, 2, 1, 0):
        panel = (c0, c1, c2, c3)[step]
        height = panel.shape[0] - R
        acc = panel[height:, :]
        if step < 3:
            acc = acc - mm(zeta[:, PANEL * (step + 1) :], panel[PANEL:height, :])
        high = acc[:, B:]
        low = acc[:, :B] - mm(high, panel[B:PANEL, :B])
        zeta[:, PANEL * step : PANEL * step + B] = low
        zeta[:, PANEL * step + B : PANEL * (step + 1)] = high
    for face in range(6):
        sends[face][...] = zeta[:, (face + 2) * B : (face + 3) * B]


def apply_kernel(map_ref, schur_ref, rhs_ref, zeta_ref, *rest):
    received, sent = rest[:6], rest[6:12]
    zeta, image, residual, gram = rest[12:16]
    sends, parts = rest[16:22], rest[22]
    rho = jnp.zeros((R, R), F32)
    for q in range(8):
        at = block(map_ref[ORDER[q]])
        local = zeta_ref[:, q * B : (q + 1) * B]
        right = rhs_ref[:, at]
        whole = local
        if q >= 2:
            right = right + sent[q - 2][B:, :]
            whole = local + received[q - 2][...]
        residual[:, at] = right
        zeta[:, at] = whole
        rho = rho + mmt(local, right)
        high = whole.astype(jnp.bfloat16)
        left = whole - high.astype(F32)
        middle = left.astype(jnp.bfloat16)
        parts[:R, at] = high
        parts[R : 2 * R, at] = middle
        parts[2 * R :, at] = (left - middle.astype(F32)).astype(jnp.bfloat16)
    full = jnp.dot(parts[...], schur_ref[...], preferred_element_type=F32)
    image[...] = full[2 * R :] + full[R : 2 * R] + full[:R]
    gram[:R, :] = rho
    gram[R:, :] = mmt(zeta[...], image[...])
    for face in range(6):
        sends[face][...] = image[:, block(map_ref[face])]


def finish_kernel(map_ref, gram_ref, zeta_ref, image_ref, residual_ref, *rest):
    received, (solution_ref, out_ref, image) = rest[:6], rest[6:]
    sub = lax.broadcasted_iota(jnp.int32, (8, 2 * R), 0)
    joined = jnp.concatenate([gram_ref[:R, :], gram_ref[R:, :]], axis=1)
    rows = [joined[8 * v : 8 * v + 8, :] for v in range(R // 8)]
    for p in range(R):
        group, s = divmod(p, 8)
        pivot = rows[group][s : s + 1, :]
        pivot = pivot / pivot[:, R + p : R + p + 1]
        new = []
        for v, old in enumerate(rows):
            out = old - old[:, R + p : R + p + 1] * pivot
            new.append(jnp.where(sub == s, pivot, out) if v == group else out)
        rows = new
    alpha = jnp.concatenate(rows, axis=0)[:, :R]
    image[...] = image_ref[...]
    for face in range(6):
        image[:, block(map_ref[face])] += received[face][...]
    solution_ref[...] = mm(alpha, zeta_ref[...], ((0,), (0,)))
    out_ref[...] = residual_ref[...] - mm(alpha, image[...], ((0,), (0,)))


def arr(*shape):
    return jax.ShapeDtypeStruct(shape, F32)


def call(kernel, outs, args, scratch=(), flops=0, name=None):
    in_specs = [SMEM if a.dtype == jnp.int32 else VMEM for a in args]
    moved = sum(a.size * a.dtype.itemsize for a in args) + sum(4 * o.size for o in outs)
    return pl.pallas_call(
        kernel,
        out_shape=outs,
        in_specs=in_specs,
        out_specs=[VMEM] * len(outs),
        scratch_shapes=scratch,
        cost_estimate=pl.CostEstimate(flops=flops, bytes_accessed=moved, transcendentals=0),
        name=name,
    )(*args)


def exchange(sends):
    received = []
    for axis, (low, high) in (("gz", sends[4:6]), ("gy", sends[2:4]), ("gx", sends[0:2])):
        up = [(i, i + 1) for i in range(lax.axis_size(axis) - 1)]
        down = [(j, i) for i, j in up]
        received = [lax.ppermute(high, axis, up), lax.ppermute(low, axis, down)] + received
    return received


def total(gram):
    nx, ny, nz = (lax.axis_size(axis) for axis in ("gx", "gy", "gz"))
    layer = [[x * nz + y + h for x in range(nx) for y in range(0, nz, 2)] for h in range(2)]
    column = [[y * nz + k + h for y in range(ny) for h in range(2)] for k in range(0, nz, 2)]

    def swap(x, axes, groups):
        return lax.all_to_all(x, axes, 0, 0, axis_index_groups=groups, tiled=True)

    pieces, depth = len(layer[0]), len(column[0])
    part = swap(gram.reshape(pieces, -1), ("gx", "gz"), layer).sum(0)
    part = swap(jnp.broadcast_to(part, (depth, part.size)), ("gy", "gz"), column).sum(0)
    whole = swap(jnp.broadcast_to(part, (pieces, part.size)), ("gx", "gz"), layer)
    return whole.reshape(gram.shape)


def shards(schur, rhs_local, block_map):
    stored = schur[0, 0, 0]
    place = block_map[0, 0, 0]
    right_side = rhs_local[0, 0, 0]
    heights = [M - PANEL * s + R for s in range(4)]
    panels = [arr(h, PANEL) for h in heights]
    inv = pltpu.VMEM((B, B), F32)

    def work(s):
        return [pltpu.VMEM((heights[s], PANEL), F32), inv]

    sends = call(
        pack_kernel, [arr(B + R, B)] * 6, (place, stored, right_side), name="pack"
    )
    met = exchange(sends)
    c0, c1, c2, c3 = call(
        first_kernel, panels, (place, stored, right_side), work(0), 10**10, "first"
    )
    c1, c2, c3 = call(
        middle_kernel, panels[1:], (c1, c2, c3, *met[:4]), work(1), 2 * 10**10, "middle"
    )
    zeta_local, *faces = call(
        last_kernel,
        [arr(R, M)] + [arr(R, B)] * 6,
        (c0, c1, c2, c3, *met[4:]),
        [pltpu.VMEM((heights[3], PANEL), F32)] + work(3),
        10**10,
        "last",
    )
    zeta_met = exchange(faces)
    zeta, image, residual, gram, *faces = call(
        apply_kernel,
        [arr(R, M)] * 3 + [arr(2 * R, R)] + [arr(R, B)] * 6,
        (place, stored, right_side, zeta_local, *zeta_met, *met),
        [pltpu.VMEM((3 * R, M), jnp.bfloat16)],
        10**9,
        "apply",
    )
    image_met = exchange(faces)
    gram = total(gram)
    solution, residual = call(
        finish_kernel,
        [arr(R, M)] * 2,
        (place, gram, zeta, image, residual, *image_met),
        [pltpu.VMEM((R, M), F32)],
        10**9,
        "finish",
    )
    return (solution[None, None, None], residual[None, None, None])


def solution(mesh):
    in_specs = (
        P("gx", "gy", "gz", None, None),
        P("gx", "gy", "gz", None, None),
        P("gx", "gy", "gz", None),
    )
    out_specs = (P("gx", "gy", "gz", None, None), P("gx", "gy", "gz", None, None))
    return jax.shard_map(shards, mesh=mesh, in_specs=in_specs, out_specs=out_specs, check_vma=False)
```

```python
import jax
import jax.numpy as jnp
from jax import lax
from jax.experimental import pallas as pl
from jax.experimental.pallas import tpu as pltpu
from jax.sharding import PartitionSpec as P


B = 128
M = 1024
R = 32
F32 = jnp.float32
HIGHEST = lax.Precision.HIGHEST
ORDER = (6, 7, 0, 1, 2, 3, 4, 5)
PANEL = 2 * B
GROUPS = 4
VMEM = pl.BlockSpec(memory_space=pltpu.VMEM)
SMEM = pl.BlockSpec(memory_space=pltpu.SMEM)


def mm(a, b, dims=((1,), (0,))):
    return lax.dot_general(
        a, b, (dims, ((), ())), precision=HIGHEST, preferred_element_type=F32
    )


def mmt(a, b):
    return mm(a, b, ((1,), (1,)))


def block(pos):
    return pl.ds(pl.multiple_of(pos * B, B), B)


def spread(row):
    return jnp.broadcast_to(row, (8, B))


def pivot_group(rows, g, lane, sub):
    base = 8 * g
    inside = (lane >= base) & (lane < base + 8)
    mine = [
        jnp.take_along_axis(rows[g], jnp.full((8, B), base + j, jnp.int32), axis=1)
        for j in range(8)
    ]
    own = jnp.where(inside, jnp.where(lane - base == sub, 1.0, 0.0), rows[g])
    for p in range(0, 8, 2):
        c0, c1 = mine[p], mine[p + 1]
        a, b, c = spread(c0[p : p + 1]), spread(c1[p : p + 1]), spread(c1[p + 1 : p + 2])
        scale = 1.0 / (a * c - b * b)
        i00, i01, i11 = c * scale, -b * scale, a * scale
        first, second = sub == p, sub == p + 1

        def clear(x):
            x0, x1 = spread(x[p : p + 1]), spread(x[p + 1 : p + 2])
            n0, n1 = i00 * x0 + i01 * x1, i01 * x0 + i11 * x1
            return jnp.where(first, n0, jnp.where(second, n1, x - c0 * n0 - c1 * n1))

        for j in range(p + 2, 8):
            mine[j] = clear(mine[j])
        own = clear(own)
    parts = [spread(own[j : j + 1]) for j in range(8)]
    new = []
    for v, old in enumerate(rows):
        out = own
        if v != g:
            out = jnp.where(inside, 0.0, old)
            for j in range(8):
                out = out - spread(old[:, base + j : base + j + 1]) * parts[j]
        new.append(out)
    return new


def inverse(rows):
    lane = lax.broadcasted_iota(jnp.int32, (8, B), 1)
    sub = lax.broadcasted_iota(jnp.int32, (8, B), 0)

    def body(_, carry):
        rows = list(carry)
        for g in range(GROUPS):
            rows = pivot_group(rows, g, lane, sub)
        rows = rows[GROUPS:] + rows[:GROUPS]
        return tuple(pltpu.roll(row, B - 8 * GROUPS, 1) for row in rows)

    return lax.fori_loop(0, 16 // GROUPS, body, tuple(rows))


def inverse_of(ref, row, col, out):
    rows = [ref[row + 8 * v : row + 8 * v + 8, col : col + B] for v in range(16)]
    for v, value in enumerate(inverse(rows)):
        out[8 * v : 8 * v + 8, :] = value


def eliminate(panel, kept, inv):
    inverse_of(panel, 0, 0, inv)
    below = panel[B:, :B]
    scaled = mm(below, inv[...])
    kept[B : panel.shape[0], :B] = below
    panel[B:, :B] = scaled
    panel[B:, B:] -= mmt(scaled, below[:B])
    inverse_of(panel, B, B, inv)
    below = panel[PANEL:, B:]
    kept[PANEL : panel.shape[0], B:] = below
    panel[PANEL:, B:] = mm(below, inv[...])


def update(panel, kept, later, gap):
    later[...] -= mmt(panel[PANEL * gap :, :], kept[PANEL * gap : PANEL * (gap + 1), :])


def pack_kernel(map_ref, schur_ref, rhs_ref, *sends):
    for face in range(6):
        at = block(map_ref[face])
        sends[face][:B, :] = schur_ref[at, at].astype(F32)
        sends[face][B:, :] = rhs_ref[:, at]


def first_kernel(map_ref, schur_ref, rhs_ref, c0, c1, c2, c3, kept, inv):
    panels = (c0, c1, c2, c3)
    for j in range(8):
        panel, left = panels[j // 2], (j % 2) * B
        col = block(map_ref[ORDER[j]])
        for i in range(j // 2 * 2, 8):
            top = (i - j // 2 * 2) * B
            panel[top : top + B, left : left + B] = schur_ref[
                block(map_ref[ORDER[i]]), col
            ].astype(F32)
        panel[panel.shape[0] - R :, left : left + B] = rhs_ref[:, col]
    eliminate(c0, kept, inv)
    for gap in (1, 2, 3):
        update(c0, kept, panels[gap], gap)


def add_received(panel, half, received):
    rows = slice(half * B, half * B + B)
    panel[rows, rows] += received[:B, :]
    panel[panel.shape[0] - R :, rows] += received[B:, :]


def middle_kernel(i1, i2, i3, x0, x1, y0, y1, c1, c2, c3, kept, inv):
    c1[...], c2[...], c3[...] = i1[...], i2[...], i3[...]
    for panel, pair in ((c1, (x0, x1)), (c2, (y0, y1))):
        for half in range(2):
            add_received(panel, half, pair[half])
    eliminate(c1, kept, inv)
    update(c1, kept, c2, 1)
    update(c1, kept, c3, 2)
    eliminate(c2, kept, inv)
    update(c2, kept, c3, 1)


def solve_back(panel, later):
    height = panel.shape[0] - R
    acc = panel[height:, :]
    if later is not None:
        acc = acc - mm(later, panel[PANEL:height, :])
    high = acc[:, B:]
    return acc[:, :B] - mm(high, panel[B:PANEL, :B]), high


def last_kernel(i3, z0, z1, low, high, c3, kept, inv):
    c3[...] = i3[...]
    add_received(c3, 0, z0)
    add_received(c3, 1, z1)
    eliminate(c3, kept, inv)
    low[...], high[...] = solve_back(c3, None)


def back_kernel(c0, c1, c2, z0, z1, zeta, *sends):
    zeta[:, 6 * B : 7 * B] = z0[...]
    zeta[:, 7 * B :] = z1[...]
    for step in (2, 1, 0):
        low, high = solve_back((c0, c1, c2)[step], zeta[:, PANEL * (step + 1) :])
        zeta[:, PANEL * step : PANEL * step + B] = low
        zeta[:, PANEL * step + B : PANEL * (step + 1)] = high
    for face in range(4):
        sends[face][...] = zeta[:, (face + 2) * B : (face + 3) * B]


def apply_kernel(map_ref, schur_ref, rhs_ref, zeta_ref, *rest):
    received, sent = rest[:6], rest[6:12]
    zeta, image, residual, gram = rest[12:16]
    sends, parts = rest[16:22], rest[22]
    rho = jnp.zeros((R, R), F32)
    for q in range(8):
        at = block(map_ref[ORDER[q]])
        local = zeta_ref[:, q * B : (q + 1) * B]
        right = rhs_ref[:, at]
        whole = local
        if q >= 2:
            right = right + sent[q - 2][B:, :]
            whole = local + received[q - 2][...]
        residual[:, at] = right
        zeta[:, at] = whole
        rho = rho + mmt(local, right)
        high = whole.astype(jnp.bfloat16)
        left = whole - high.astype(F32)
        middle = left.astype(jnp.bfloat16)
        parts[:R, at] = high
        parts[R : 2 * R, at] = middle
        parts[2 * R :, at] = (left - middle.astype(F32)).astype(jnp.bfloat16)
    full = jnp.dot(parts[...], schur_ref[...], preferred_element_type=F32)
    image[...] = full[2 * R :] + full[R : 2 * R] + full[:R]
    gram[:R, :] = rho
    gram[R:, :] = mmt(zeta[...], image[...])
    for face in range(6):
        sends[face][...] = image[:, block(map_ref[face])]


def finish_kernel(map_ref, gram_ref, zeta_ref, image_ref, residual_ref, *rest):
    received, (solution_ref, out_ref, image) = rest[:6], rest[6:]
    sub = lax.broadcasted_iota(jnp.int32, (8, 2 * R), 0)
    joined = jnp.concatenate([gram_ref[:R, :], gram_ref[R:, :]], axis=1)
    rows = [joined[8 * v : 8 * v + 8, :] for v in range(R // 8)]
    for p in range(R):
        group, s = divmod(p, 8)
        pivot = rows[group][s : s + 1, :]
        pivot = pivot / pivot[:, R + p : R + p + 1]
        new = []
        for v, old in enumerate(rows):
            out = old - old[:, R + p : R + p + 1] * pivot
            new.append(jnp.where(sub == s, pivot, out) if v == group else out)
        rows = new
    alpha = jnp.concatenate(rows, axis=0)[:, :R]
    image[...] = image_ref[...]
    for face in range(6):
        image[:, block(map_ref[face])] += received[face][...]
    solution_ref[...] = mm(alpha, zeta_ref[...], ((0,), (0,)))
    out_ref[...] = residual_ref[...] - mm(alpha, image[...], ((0,), (0,)))


def arr(*shape):
    return jax.ShapeDtypeStruct(shape, F32)


def call(kernel, outs, args, scratch=(), flops=0):
    in_specs = [SMEM if a.dtype == jnp.int32 else VMEM for a in args]
    moved = sum(a.size * a.dtype.itemsize for a in args) + sum(4 * o.size for o in outs)
    return pl.pallas_call(
        kernel,
        out_shape=outs,
        in_specs=in_specs,
        out_specs=[VMEM] * len(outs),
        scratch_shapes=scratch,
        cost_estimate=pl.CostEstimate(flops=flops, bytes_accessed=moved, transcendentals=0),
    )(*args)


def exchange(axis, low, high):
    up = [(i, i + 1) for i in range(lax.axis_size(axis) - 1)]
    down = [(j, i) for i, j in up]
    before = lax.ppermute(high, axis, up)
    after = lax.ppermute(low, axis, down)
    return before, after


def exchange_all(sends):
    along_z = exchange("gz", *sends[4:])
    return *exchange("gx", *sends[:2]), *exchange("gy", *sends[2:4]), *along_z


def total(gram):
    nx, ny, nz = (lax.axis_size(axis) for axis in ("gx", "gy", "gz"))
    layer = [[x * nz + y + h for x in range(nx) for y in range(0, nz, 2)] for h in range(2)]
    column = [[y * nz + k + h for y in range(ny) for h in range(2)] for k in range(0, nz, 2)]

    def swap(x, axes, groups):
        return lax.all_to_all(x, axes, 0, 0, axis_index_groups=groups, tiled=True)

    pieces, depth = len(layer[0]), len(column[0])
    part = swap(gram.reshape(pieces, -1), ("gx", "gz"), layer).sum(0)
    part = swap(jnp.broadcast_to(part, (depth, part.size)), ("gy", "gz"), column).sum(0)
    whole = swap(jnp.broadcast_to(part, (pieces, part.size)), ("gx", "gz"), layer)
    return whole.reshape(gram.shape)


def step(schur, rhs_local, block_map):
    stored = schur[0, 0, 0]
    place = block_map[0, 0, 0]
    right_side = rhs_local[0, 0, 0]
    heights = [M - PANEL * s + R for s in range(4)]
    panels = [arr(h, PANEL) for h in heights]
    inv = pltpu.VMEM((B, B), F32)

    def work(s):
        return [pltpu.VMEM((heights[s], PANEL), F32), inv]

    sends = call(pack_kernel, [arr(B + R, B)] * 6, (place, stored, right_side))
    met = exchange_all(sends)
    c0, c1, c2, c3 = call(first_kernel, panels, (place, stored, right_side), work(0), 10**10)
    c1, c2, c3 = call(middle_kernel, panels[1:], (c1, c2, c3, *met[:4]), work(1), 2 * 10**10)
    z_faces = call(
        last_kernel,
        [arr(R, B)] * 2,
        (c3, *met[4:]),
        [pltpu.VMEM((heights[3], PANEL), F32)] + work(3),
        10**10,
    )
    z_met = exchange("gz", *z_faces)
    zeta_local, *faces = call(
        back_kernel, [arr(R, M)] + [arr(R, B)] * 4, (c0, c1, c2, *z_faces), (), 10**9
    )
    zeta_met = (*exchange("gx", *faces[:2]), *exchange("gy", *faces[2:]), *z_met)
    zeta, image, residual, gram, *faces = call(
        apply_kernel,
        [arr(R, M)] * 3 + [arr(2 * R, R)] + [arr(R, B)] * 6,
        (place, stored, right_side, zeta_local, *zeta_met, *met),
        [pltpu.VMEM((3 * R, M), jnp.bfloat16)],
        10**9,
    )
    image_met = exchange_all(faces)
    gram = total(gram)
    solution, residual = call(
        finish_kernel,
        [arr(R, M)] * 2,
        (place, gram, zeta, image, residual, *image_met),
        [pltpu.VMEM((R, M), F32)],
        10**9,
    )
    return (solution[None, None, None], residual[None, None, None])


def solution(mesh):
    in_specs = (
        P("gx", "gy", "gz", None, None),
        P("gx", "gy", "gz", None, None),
        P("gx", "gy", "gz", None),
    )
    out_specs = (P("gx", "gy", "gz", None, None), P("gx", "gy", "gz", None, None))
    return jax.shard_map(step, mesh=mesh, in_specs=in_specs, out_specs=out_specs, check_vma=False)
```

```python
import jax
import jax.numpy as jnp
from jax import lax
from jax.experimental import pallas as pl
from jax.experimental.pallas import tpu as pltpu
from jax.sharding import PartitionSpec as P


B = 128
M = 1024
R = 32
F32 = jnp.float32
HIGHEST = lax.Precision.HIGHEST
ORDER = (6, 7, 0, 1, 2, 3, 4, 5)
PANEL = 2 * B
GROUPS = 4
VMEM = pl.BlockSpec(memory_space=pltpu.VMEM)
SMEM = pl.BlockSpec(memory_space=pltpu.SMEM)


def mm(a, b, dims=((1,), (0,))):
    return lax.dot_general(
        a, b, (dims, ((), ())), precision=HIGHEST, preferred_element_type=F32
    )


def mmt(a, b):
    return mm(a, b, ((1,), (1,)))


def block(pos):
    return pl.ds(pl.multiple_of(pos * B, B), B)


def spread(row):
    return jnp.broadcast_to(row, (8, B))


def clear_pivots(row, own, base, sub):
    mine = [
        jnp.take_along_axis(row, jnp.full((8, B), base + j, jnp.int32), axis=1) for j in range(8)
    ]
    for p in range(0, 8, 2):
        c0, c1 = mine[p], mine[p + 1]
        a, b, c = spread(c0[p : p + 1]), spread(c1[p : p + 1]), spread(c1[p + 1 : p + 2])
        scale = 1.0 / (a * c - b * b)
        i00, i01, i11 = c * scale, -b * scale, a * scale
        first, second = sub == p, sub == p + 1

        def clear(x):
            x0, x1 = spread(x[p : p + 1]), spread(x[p + 1 : p + 2])
            n0, n1 = i00 * x0 + i01 * x1, i01 * x0 + i11 * x1
            return jnp.where(first, n0, jnp.where(second, n1, x - c0 * n0 - c1 * n1))

        for j in range(p + 2, 8):
            mine[j] = clear(mine[j])
        own = clear(own)
    return own


def clear_rows(rows, which, own, base, inside=None):
    old = {v: rows[v] for v in which}
    if inside is not None:
        for v in which:
            rows[v] = jnp.where(inside, 0.0, rows[v])
    for j in range(8):
        part = spread(own[j : j + 1])
        for v in which:
            rows[v] = rows[v] - spread(old[v][:, base + j : base + j + 1]) * part


def sweep(rows, groups, start, lane, sub, exchange_pivots):
    for g in range(groups):
        base = start + 8 * g
        own, inside = rows[g], None
        if exchange_pivots:
            inside = (lane >= base) & (lane < base + 8)
            own = jnp.where(inside, jnp.where(lane - base == sub, 1.0, 0.0), own)
        rows[g] = clear_pivots(rows[g], own, base, sub)
        others = [v for v in range(len(rows)) if v != g]
        clear_rows(rows, others, rows[g], base, inside)
    return rows


def iotas():
    return (lax.broadcasted_iota(jnp.int32, (8, B), axis) for axis in (1, 0))


def inverse(rows):
    lane, sub = iotas()

    def body(_, carry):
        rows = sweep(list(carry), GROUPS, 0, lane, sub, True)
        rows = rows[GROUPS:] + rows[:GROUPS]
        return tuple(pltpu.roll(row, B - 8 * GROUPS, 1) for row in rows)

    return lax.fori_loop(0, 16 // GROUPS, body, tuple(rows))


def inverse_of(ref, row, col, out):
    rows = [ref[row + 8 * v : row + 8 * v + 8, col : col + B] for v in range(16)]
    for v, value in enumerate(inverse(rows)):
        out[8 * v : 8 * v + 8, :] = value


def eliminate(panel, kept, inv):
    inverse_of(panel, 0, 0, inv)
    below = panel[B:, :B]
    scaled = mm(below, inv[...])
    kept[B : panel.shape[0], :B] = below
    panel[B:, :B] = scaled
    panel[B:, B:] -= mmt(scaled, below[:B])
    inverse_of(panel, B, B, inv)
    below = panel[PANEL:, B:]
    kept[PANEL : panel.shape[0], B:] = below
    panel[PANEL:, B:] = mm(below, inv[...])


def update(panel, kept, later, gap):
    later[...] -= mmt(panel[PANEL * gap :, :], kept[PANEL * gap : PANEL * (gap + 1), :])


def pack_kernel(map_ref, schur_ref, rhs_ref, *sends):
    for face in range(6):
        at = block(map_ref[face])
        sends[face][:B, :] = schur_ref[at, at].astype(F32)
        sends[face][B:, :] = rhs_ref[:, at]


def first_kernel(map_ref, schur_ref, rhs_ref, c0, c1, c2, c3, kept, inv):
    panels = (c0, c1, c2, c3)
    for j in range(8):
        panel, left = panels[j // 2], (j % 2) * B
        col = block(map_ref[ORDER[j]])
        for i in range(j // 2 * 2, 8):
            top = (i - j // 2 * 2) * B
            panel[top : top + B, left : left + B] = schur_ref[
                block(map_ref[ORDER[i]]), col
            ].astype(F32)
        panel[panel.shape[0] - R :, left : left + B] = rhs_ref[:, col]
    eliminate(c0, kept, inv)
    for gap in (1, 2, 3):
        update(c0, kept, panels[gap], gap)


def add_received(panel, half, received):
    rows = slice(half * B, half * B + B)
    panel[rows, rows] += received[:B, :]
    panel[panel.shape[0] - R :, rows] += received[B:, :]


def middle_kernel(i1, i2, i3, x0, x1, y0, y1, c1, c2, c3, kept, inv):
    c1[...], c2[...], c3[...] = i1[...], i2[...], i3[...]
    for panel, pair in ((c1, (x0, x1)), (c2, (y0, y1))):
        for half in range(2):
            add_received(panel, half, pair[half])
    eliminate(c1, kept, inv)
    update(c1, kept, c2, 1)
    update(c1, kept, c3, 2)
    eliminate(c2, kept, inv)
    update(c2, kept, c3, 1)


def solve_back(panel, later):
    height = panel.shape[0] - R
    acc = panel[height:, :]
    if later is not None:
        acc = acc - mm(later, panel[PANEL:height, :])
    high = acc[:, B:]
    return acc[:, :B] - mm(high, panel[B:PANEL, :B]), high


def last_kernel(i3, z0, z1, low, high, c3, kept, inv):
    c3[...] = i3[...]
    add_received(c3, 0, z0)
    add_received(c3, 1, z1)
    eliminate(c3, kept, inv)
    low[...], high[...] = solve_back(c3, None)


def back_kernel(c0, c1, c2, z0, z1, zeta, *sends):
    zeta[:, 6 * B : 7 * B] = z0[...]
    zeta[:, 7 * B :] = z1[...]
    for step in (2, 1, 0):
        low, high = solve_back((c0, c1, c2)[step], zeta[:, PANEL * (step + 1) :])
        zeta[:, PANEL * step : PANEL * step + B] = low
        zeta[:, PANEL * step + B : PANEL * (step + 1)] = high
    for face in range(4):
        sends[face][...] = zeta[:, (face + 2) * B : (face + 3) * B]


def apply_kernel(map_ref, schur_ref, rhs_ref, zeta_ref, *rest):
    received, sent = rest[:6], rest[6:12]
    zeta, image, residual, gram = rest[12:16]
    sends, parts = rest[16:22], rest[22]
    rho = jnp.zeros((R, R), F32)
    for q in range(8):
        at = block(map_ref[ORDER[q]])
        local = zeta_ref[:, q * B : (q + 1) * B]
        right = rhs_ref[:, at]
        whole = local
        if q >= 2:
            right = right + sent[q - 2][B:, :]
            whole = local + received[q - 2][...]
        residual[:, at] = right
        zeta[:, at] = whole
        rho = rho + mmt(local, right)
        high = whole.astype(jnp.bfloat16)
        left = whole - high.astype(F32)
        middle = left.astype(jnp.bfloat16)
        parts[:R, at] = high
        parts[R : 2 * R, at] = middle
        parts[2 * R :, at] = (left - middle.astype(F32)).astype(jnp.bfloat16)
    full = jnp.dot(parts[...], schur_ref[...], preferred_element_type=F32)
    image[...] = full[2 * R :] + full[R : 2 * R] + full[:R]
    gram[:, :R] = rho
    gram[:, R:] = mmt(zeta[...], image[...])
    for face in range(6):
        sends[face][...] = image[:, block(map_ref[face])]


def finish_kernel(map_ref, gram_ref, zeta_ref, image_ref, residual_ref, *rest):
    received, (solution_ref, out_ref, image, joined) = rest[:6], rest[6:]
    lane, sub = iotas()
    joined[...] = jnp.zeros((R, B), F32)
    joined[:, : 2 * R] = gram_ref[...]
    rows = [joined[8 * v : 8 * v + 8, :] for v in range(R // 8)]
    rows = sweep(rows, R // 8, R, lane, sub, False)
    alpha = jnp.concatenate(rows, axis=0)[:, :R]
    image[...] = image_ref[...]
    for face in range(6):
        image[:, block(map_ref[face])] += received[face][...]
    solution_ref[...] = mm(alpha, zeta_ref[...], ((0,), (0,)))
    out_ref[...] = residual_ref[...] - mm(alpha, image[...], ((0,), (0,)))


def arr(*shape):
    return jax.ShapeDtypeStruct(shape, F32)


def call(kernel, outs, args, scratch=(), flops=0):
    in_specs = [SMEM if a.dtype == jnp.int32 else VMEM for a in args]
    moved = sum(a.size * a.dtype.itemsize for a in args) + sum(4 * o.size for o in outs)
    return pl.pallas_call(
        kernel,
        out_shape=outs,
        in_specs=in_specs,
        out_specs=[VMEM] * len(outs),
        scratch_shapes=scratch,
        cost_estimate=pl.CostEstimate(flops=flops, bytes_accessed=moved, transcendentals=0),
    )(*args)


def exchange(axis, low, high):
    up = [(i, i + 1) for i in range(lax.axis_size(axis) - 1)]
    down = [(j, i) for i, j in up]
    before = lax.ppermute(high, axis, up)
    after = lax.ppermute(low, axis, down)
    return before, after


def exchange_all(sends):
    along_z = exchange("gz", *sends[4:])
    return *exchange("gx", *sends[:2]), *exchange("gy", *sends[2:4]), *along_z


def total(gram):
    nx, ny, nz = (lax.axis_size(axis) for axis in ("gx", "gy", "gz"))
    layer = [[x * nz + y + h for x in range(nx) for y in range(0, nz, 2)] for h in range(2)]
    column = [[y * nz + k + h for y in range(ny) for h in range(2)] for k in range(0, nz, 2)]

    def swap(x, axes, groups):
        return lax.all_to_all(x, axes, 0, 0, axis_index_groups=groups, tiled=True)

    pieces, depth = len(layer[0]), len(column[0])
    part = swap(gram.reshape(pieces, -1), ("gx", "gz"), layer).sum(0)
    part = swap(jnp.broadcast_to(part, (depth, part.size)), ("gy", "gz"), column).sum(0)
    whole = swap(jnp.broadcast_to(part, (pieces, part.size)), ("gx", "gz"), layer)
    return whole.reshape(gram.shape)


def step(schur, rhs_local, block_map):
    stored = schur[0, 0, 0]
    place = block_map[0, 0, 0]
    right_side = rhs_local[0, 0, 0]
    heights = [M - PANEL * s + R for s in range(4)]
    panels = [arr(h, PANEL) for h in heights]
    inv = pltpu.VMEM((B, B), F32)

    def work(s):
        return [pltpu.VMEM((heights[s], PANEL), F32), inv]

    sends = call(pack_kernel, [arr(B + R, B)] * 6, (place, stored, right_side))
    met = exchange_all(sends)
    c0, c1, c2, c3 = call(first_kernel, panels, (place, stored, right_side), work(0), 10**10)
    c1, c2, c3 = call(middle_kernel, panels[1:], (c1, c2, c3, *met[:4]), work(1), 2 * 10**10)
    z_faces = call(
        last_kernel,
        [arr(R, B)] * 2,
        (c3, *met[4:]),
        [pltpu.VMEM((heights[3], PANEL), F32)] + work(3),
        10**10,
    )
    z_met = exchange("gz", *z_faces)
    zeta_local, *faces = call(
        back_kernel, [arr(R, M)] + [arr(R, B)] * 4, (c0, c1, c2, *z_faces), (), 10**9
    )
    zeta_met = (*exchange("gx", *faces[:2]), *exchange("gy", *faces[2:]), *z_met)
    zeta, image, residual, gram, *faces = call(
        apply_kernel,
        [arr(R, M)] * 3 + [arr(R, 2 * R)] + [arr(R, B)] * 6,
        (place, stored, right_side, zeta_local, *zeta_met, *met),
        [pltpu.VMEM((3 * R, M), jnp.bfloat16)],
        10**9,
    )
    image_met = exchange_all(faces)
    gram = total(gram)
    solution, residual = call(
        finish_kernel,
        [arr(R, M)] * 2,
        (place, gram, zeta, image, residual, *image_met),
        [pltpu.VMEM((R, M), F32), pltpu.VMEM((R, B), F32)],
        10**9,
    )
    return (solution[None, None, None], residual[None, None, None])


def solution(mesh):
    in_specs = (
        P("gx", "gy", "gz", None, None),
        P("gx", "gy", "gz", None, None),
        P("gx", "gy", "gz", None),
    )
    out_specs = (P("gx", "gy", "gz", None, None), P("gx", "gy", "gz", None, None))
    return jax.shard_map(step, mesh=mesh, in_specs=in_specs, out_specs=out_specs, check_vma=False)
```
